32 devices in a mesh: frame: 8 (over z, core), tok: 4 (over y, x).
Axes of the slice: x: 2, y: 2, z: 4, core: 2. Of those that a mesh axis runs over, the one named last changes fastest.
Arguments:
- stream: bfloat16 [8, 1024, 1152], P('frame', 'tok'), may hold values from -20 to 20
- queries: bfloat16 [8, 1024, 1152], P('frame', 'tok'), may hold values from -200 to 200
- key_vectors: bfloat16 [8, 1024, 1152], P('frame', 'tok'), may hold values from -6 to 6
- value_vectors: bfloat16 [8, 1024, 1152], P('frame', 'tok'), may hold values from -6 to 6
- modulation: float32 [8, 4, 1152], P('frame'), may hold values from -4 to 4
- output_weight: bfloat16 [1152, 1152], replicated, may hold values from -0.1875 to 0.1875
- output_bias: float32 [1152], replicated, may hold values from -3 to 3
- router_weight: bfloat16 [1152, 8], replicated, may hold values from -0.1875 to 0.1875
- expand_weight: bfloat16 [8, 1152, 4608], P('frame', None, 'tok'), may hold values from -0.1875 to 0.1875
- expand_bias: float32 [8, 4608], P('frame', 'tok'), may hold values from -3 to 3
- reduce_weight: bfloat16 [8, 4608, 1152], P('frame', 'tok'), may hold values from -0.09375 to 0.09375
- reduce_bias: float32 [8, 1152], P('frame'), may hold values from -3 to 3
- counts: int32 [8, 8], P(None, 'frame'), may hold values from 1 to 96, 256 in all within a row
- picked_rows: int32 [8, 8, 96], P(None, 'frame'), may hold values from 0 to 1023, as said below
Outputs:
- layer_out: bfloat16 [8, 1024, 1152], P('frame', 'tok')
The draws below stay inside these ranges and needn't reach their ends.
Inputs may be any that keep to these rules, and one draw needn't show every extreme that they name: counts[e, g] slots of block (e, g) are used; the counts of one expert sum to 256. The entries of one block picked_rows[e, g, :] are distinct positions among the 1024 tokens of frame g; slots at or beyond counts[e, g] are unused.
All inputs are finite; a program needn't handle non-finite values.
Results may differ from the reference program's by a relative error of at most 0.0055.
Values may be sent and summed in bfloat16 or wider, within the bound.
A program may use at most 64 MiB of HBM per device.

```python
import math
import jax
import jax.numpy as jnp
import numpy as np
from jax import lax

D = 1152
H = 16
HD = 72
FF = 4608
CAP = 256
FTOK = 1024
FRAMES = 8
EXPERTS = 8
BLK = 96
N_FRAME = 8


def draw_stream(key, part):
    first_key, second_key = jax.random.split(key, 2)
    column_scale = jnp.exp(jax.random.uniform(second_key, (1, 1, D), jnp.float32, math.log(0.3), math.log(3.0)))
    values = jax.random.normal(first_key, (FRAMES, FTOK, D), jnp.float32) * column_scale
    return jnp.clip(values, -20.0, 20.0).astype(jnp.bfloat16)


def drawn_pair(key):
    key_draw = jnp.clip(jax.random.normal(jax.random.fold_in(key, 17), (FRAMES, FTOK, D), jnp.float32), -6.0, 6.0)
    query_draw = jnp.clip(2.5 * jax.random.normal(jax.random.fold_in(key, 29), (FRAMES, FTOK, D), jnp.float32), -15.0, 15.0)
    return (query_draw, key_draw)


def draw_queries(key, part):
    query_draw, key_draw = drawn_pair(key)
    return query_draw.astype(jnp.bfloat16)


def draw_key_vectors(key, part):
    query_draw, key_draw = drawn_pair(key)
    return key_draw.astype(jnp.bfloat16)


def draw_picked_rows(key, part):
    block_keys = jax.random.split(key, EXPERTS * N_FRAME)

    def one_block(block_key):
        return jax.random.permutation(block_key, FTOK)[:BLK].astype(jnp.int32)
    picked = jax.vmap(one_block)(block_keys).reshape(EXPERTS, N_FRAME, BLK)
    upper = (picked[0, 0] - picked[0, 0, 0] + FTOK - 1) % FTOK
    lower = (picked[0, 1] - picked[0, 1, 0]) % FTOK
    picked = picked.at[0, 0].set(upper.astype(jnp.int32))
    picked = picked.at[0, 1].set(lower.astype(jnp.int32))
    return picked.astype(jnp.int32)


def block_levels(own_key, shape, shards, least, high):
    def one(axis_at, shards_of):
        steps = jax.random.uniform(jax.random.fold_in(jax.random.fold_in(own_key, 6), axis_at), (shards_of,), jnp.float32, least / len(shards), high / len(shards))
        return jnp.repeat(jnp.exp(steps), shape[axis_at] // shards_of).reshape((-1,) + (1,) * (len(shape) - axis_at - 1))

    level = one(*shards[0])
    for cut in shards[1:]:
        level = level * one(*cut)
    return level


def split_up(count, total, bound, slope):
    portions = [(1 << 20) // math.isqrt(rank ** slope) + 1 for rank in range(2, count + 1)]
    rest, given = total - bound - (count - 1), [1] * (count - 1)
    while rest > 0:
        free = [i for i in range(count - 1) if given[i] < bound]
        whole, budget = sum([portions[i] for i in free]), rest
        for i in free:
            more = min(bound - given[i], max(1, budget * portions[i] // whole), rest)
            given[i] = given[i] + more
            rest = rest - more
    return np.array([bound] + given)


def ragged_sizes(own_key, number_of, total, most, lean):
    if number_of == 2:
        one = jax.random.randint(own_key, (), max(1, total - most), min(most, total - 1) + 1)
        return jnp.stack([one, total - one])
    lengths = jnp.asarray(split_up(number_of, total, most, lean), jnp.int32)
    twos = (number_of - 1) // 2
    donor, receiver = lengths[1:1 + 2 * twos:2], lengths[2:2 + 2 * twos:2]
    room = jnp.minimum(donor - 1, most - receiver)
    passed = jax.random.randint(jax.random.fold_in(own_key, 1), (twos,), 0, 1 << 20) % (room + 1)
    lengths = lengths.at[1:1 + 2 * twos:2].set(donor - passed).at[2:2 + 2 * twos:2].set(receiver + passed)
    return lengths[jax.random.permutation(jax.random.fold_in(own_key, 2), number_of)]


def noise(own_key, shape, spread, most, cuts=(), kind=jnp.bfloat16):
    array = spread * jax.random.normal(own_key, shape, jnp.float32)
    if cuts:
        array = array * block_levels(own_key, shape, cuts, -0.22, 0.18)
    return jnp.clip(array, -most, most).astype(kind)


def setup_inputs(seed: int = 0) -> dict:
    keys = jax.random.split(jax.random.key(seed), 15)
    stream = draw_stream(jax.random.fold_in(keys[14], 71), 0)
    queries = draw_queries(jax.random.fold_in(keys[14], 71), 0)
    key_vectors = draw_key_vectors(jax.random.fold_in(keys[14], 71), 0)
    value_vectors = noise(keys[3], (FRAMES, FTOK, D), 1.0, 6.0, ((0, 8), (1, 4)))
    modulation = noise(keys[4], (FRAMES, 4, D), 1.0, 4.0, ((0, 8),), jnp.float32)
    output_weight = noise(keys[5], (D, D), D ** -0.5, 0.1875)
    output_bias = noise(keys[6], (D,), 0.5, 3.0, (), jnp.float32)
    router_weight = noise(keys[7], (D, EXPERTS), D ** -0.5, 0.1875)
    expand_weight = noise(keys[8], (EXPERTS, D, FF), D ** -0.5, 0.1875, ((0, 8), (2, 4)))
    expand_bias = noise(keys[9], (EXPERTS, FF), 0.5, 3.0, ((0, 8), (1, 4)), jnp.float32)
    reduce_weight = noise(keys[10], (EXPERTS, FF, D), FF ** -0.5, 0.09375, ((0, 8), (1, 4)))
    reduce_bias = noise(keys[11], (EXPERTS, D), 0.5, 3.0, ((0, 8),), jnp.float32)
    counts = jax.vmap(lambda own: ragged_sizes(own, N_FRAME, CAP, BLK, 2))(jax.random.split(keys[12], EXPERTS)).reshape((EXPERTS, N_FRAME)).astype(jnp.int32)
    picked_rows = draw_picked_rows(jax.random.fold_in(keys[14], 71), 0)
    return {"stream": stream, "queries": queries, "key_vectors": key_vectors, "value_vectors": value_vectors, "modulation": modulation, "output_weight": output_weight, "output_bias": output_bias, "router_weight": router_weight, "expand_weight": expand_weight, "expand_bias": expand_bias, "reduce_weight": reduce_weight, "reduce_bias": reduce_bias, "counts": counts, "picked_rows": picked_rows}


def layer_norm(values):
    mean_val = lax.optimization_barrier(jnp.mean(values, axis=-1, keepdims=True))
    centred = values - mean_val
    variance = lax.optimization_barrier(jnp.mean(centred * centred, axis=-1, keepdims=True))
    return centred * lax.rsqrt(variance + 1e-06)

def head_attention(operands):
    head_queries, head_keys, head_values = operands
    scores = jnp.dot(head_queries, head_keys.T, preferred_element_type=jnp.float32) * (1.0 / math.sqrt(HD))
    scores = scores - lax.optimization_barrier(jnp.max(scores, axis=-1, keepdims=True))
    exponent = jnp.exp(scores)
    weights = (exponent / lax.optimization_barrier(jnp.sum(exponent, axis=-1, keepdims=True))).astype(jnp.bfloat16)
    return jnp.dot(weights, head_values, preferred_element_type=jnp.float32).astype(jnp.bfloat16)

def split_heads(tensor):
    return tensor.reshape(FRAMES, FTOK, H, HD).transpose(0, 2, 1, 3).reshape(FRAMES * H, FTOK, HD)

def reference(stream, queries, key_vectors, value_vectors, modulation, output_weight, output_bias, router_weight, expand_weight, expand_bias, reduce_weight, reduce_bias, counts, picked_rows):
    attended = lax.map(head_attention, (split_heads(queries), split_heads(key_vectors), split_heads(value_vectors)))
    attended = attended.reshape(FRAMES, H, FTOK, HD).transpose(0, 2, 1, 3).reshape(FRAMES * FTOK, D)
    projected = jnp.dot(attended, output_weight, preferred_element_type=jnp.float32) + output_bias
    projected = projected.reshape(FRAMES, FTOK, D)
    residual = (stream.astype(jnp.float32) + modulation[:, 0:1, :] * projected).astype(jnp.bfloat16)
    normed = layer_norm(residual.astype(jnp.float32)) * (1.0 + modulation[:, 2:3, :]) + modulation[:, 1:2, :]
    normed = normed.astype(jnp.bfloat16)
    gate_values = jax.nn.sigmoid(jnp.dot(normed.reshape(FRAMES * FTOK, D), router_weight, preferred_element_type=jnp.float32)).reshape(FRAMES, FTOK, EXPERTS)
    slot_ids = jnp.arange(BLK, dtype=jnp.int32)
    in_use_all = slot_ids[None, None, :] < counts[:, :, None]
    frame_ids = jnp.arange(FRAMES, dtype=jnp.int32)[:, None]

    def one_expert(total, operands):
        expert_id, row_index, in_use, expand_one, expand_bias_one, reduce_one, reduce_bias_one = operands
        chosen = normed[frame_ids, row_index]
        chosen = jnp.where(in_use[:, :, None], chosen, jnp.zeros_like(chosen)).reshape(FRAMES * BLK, D)
        hidden = jax.nn.gelu(jnp.dot(chosen, expand_one, preferred_element_type=jnp.float32) + expand_bias_one, approximate=True).astype(jnp.bfloat16)
        expert_out = (jnp.dot(hidden, reduce_one, preferred_element_type=jnp.float32) + reduce_bias_one).astype(jnp.bfloat16)
        mix_weight = gate_values[frame_ids, row_index, expert_id]
        mix_weight = jnp.where(in_use, mix_weight, jnp.zeros_like(mix_weight)).astype(jnp.bfloat16)
        term = mix_weight.astype(jnp.float32)[:, :, None] * expert_out.reshape(FRAMES, BLK, D).astype(jnp.float32)
        total = total.at[frame_ids, row_index].add(term)
        return (total, None)
    expert_ids = jnp.arange(EXPERTS, dtype=jnp.int32)
    expert_mix, unused = lax.scan(one_expert, jnp.zeros((FRAMES, FTOK, D), jnp.float32), (expert_ids, picked_rows, in_use_all, expand_weight, expand_bias, reduce_weight, reduce_bias))
    return (residual.astype(jnp.float32) + modulation[:, 3:4, :] * expert_mix).astype(jnp.bfloat16)
```

```python
import functools
import math

import jax
import jax.numpy as jnp
from jax import lax
from jax.experimental import pallas as pl
from jax.experimental.pallas import tpu as pltpu
from jax.sharding import PartitionSpec as P

H = 16
HD = 72
CAP = 256
BF = jnp.bfloat16
F32 = jnp.float32


def dot(a, b, ca, cb):
    return lax.dot_general(a, b, (((ca,), (cb,)), ((), ())), preferred_element_type=F32)


def attention_kernel(q_ref, k_ref, v_ref, o_ref):
    sources = q_ref.shape[0]
    scale = math.log2(math.e) / math.sqrt(HD)
    keys = jnp.concatenate([k_ref[s, 0] for s in range(sources)], axis=1).T
    values = jnp.concatenate([v_ref[s, 0] for s in range(sources)], axis=1)

    def block(j, carry):
        scores = dot(keys, q_ref[j, 0], 1, 0)
        top = jnp.max(scores, axis=0, keepdims=True)
        powers = jnp.exp2((scores - top) * scale)
        total = jnp.sum(powers, axis=0, keepdims=True)
        out = dot(values, powers.astype(BF), 1, 0)
        o_ref[j, 0] = (out / total).astype(BF)
        return carry

    lax.fori_loop(0, sources, block, 0)


def attention(q, k, v):
    sources, heads, _, tokens = q.shape
    spec = pl.BlockSpec((sources, 1, HD, tokens), lambda h: (0, h, 0, 0))
    return pl.pallas_call(
        attention_kernel,
        out_shape=jax.ShapeDtypeStruct(q.shape, BF),
        grid=(heads,),
        in_specs=[spec] * 3,
        out_specs=spec,
        compiler_params=pltpu.CompilerParams(vmem_limit_bytes=48 << 20),
    )(q, k, v)


def swap(x, axis):
    return lax.all_to_all(x, axis, split_axis=0, concat_axis=0, tiled=True)


def per_device(
    stream,
    queries,
    key_vectors,
    value_vectors,
    modulation,
    output_weight,
    output_bias,
    router_weight,
    expand_weight,
    expand_bias,
    reduce_weight,
    reduce_bias,
    counts,
    picked_rows,
):
    shards = lax.axis_size("tok")
    tokens = stream.shape[1]
    width = stream.shape[2]
    cols = width // shards
    heads = H // shards
    experts, _, slots = picked_rows.shape
    frame_tokens = tokens * shards

    def to_heads(x):
        return swap(x[0].T.reshape(shards, heads, HD, tokens), "tok")

    attended = attention(to_heads(queries), to_heads(key_vectors), to_heads(value_vectors))
    attended = swap(attended, "tok").reshape(width, tokens)
    shares = modulation[0].T
    projected = dot(output_weight, attended, 0, 0) + output_bias[:, None]
    residual = (stream[0].T.astype(F32) + shares[:, 0:1] * projected).astype(BF)
    wide = residual.astype(F32)
    centred = wide - jnp.mean(wide, axis=0, keepdims=True)
    variance = jnp.mean(centred * centred, axis=0, keepdims=True)
    normed = (
        centred * lax.rsqrt(variance + 1e-06) * (1.0 + shares[:, 2:3]) + shares[:, 1:2]
    ).astype(BF)
    gates = jax.nn.sigmoid(dot(router_weight, normed, 0, 0)).astype(BF)
    sent = jnp.concatenate(
        [
            normed.reshape(shards, cols, tokens),
            jnp.broadcast_to(gates[None], (shards, experts, tokens)),
        ],
        axis=1,
    )
    held = swap(sent, "tok").transpose(1, 0, 2).reshape(cols + experts, frame_tokens)
    used = jnp.arange(slots, dtype=jnp.int32)[None, :] < counts
    where_to = jnp.where(used, picked_rows[:, 0, :], -1)
    hits = where_to[:, :, None] == jnp.arange(frame_tokens, dtype=jnp.int32)[None, None, :]
    pick = hits.astype(BF).reshape(experts * slots, frame_tokens)
    chosen = dot(pick, held[:cols], 1, 1).astype(BF)
    arrived = swap(chosen.reshape(experts, slots, cols), "frame").reshape(-1, cols)
    own_counts = swap(counts, "frame")[:, 0]
    first = jnp.cumsum(own_counts) - own_counts
    slot = jnp.arange(slots, dtype=jnp.int32)[None, :]
    row = jnp.where(slot < own_counts[:, None], first[:, None] + slot, -1).reshape(-1)
    pack = (jnp.arange(CAP, dtype=jnp.int32)[:, None] == row[None, :]).astype(BF)
    rows = dot(pack, arrived, 1, 0).astype(BF)
    all_rows = swap(jnp.broadcast_to(rows[None], (shards, CAP, cols)), "tok")
    all_rows = all_rows.transpose(1, 0, 2).reshape(CAP, width)
    hidden = jax.nn.gelu(
        dot(all_rows, expand_weight[0], 1, 0) + expand_bias, approximate=True
    ).astype(BF)
    partial_out = dot(hidden, reduce_weight[0], 1, 0).astype(BF)
    pieces = swap(partial_out.reshape(CAP, shards, cols).transpose(1, 0, 2), "tok")
    bias = lax.dynamic_slice_in_dim(reduce_bias, lax.axis_index("tok") * cols, cols, 1)
    expert_out = (jnp.sum(pieces.astype(F32), axis=0) + bias).astype(BF)
    spread = dot(pack, expert_out, 0, 0).astype(BF)
    returned = swap(spread.reshape(-1, slots, cols), "frame").reshape(-1, cols)
    table = jnp.where(hits, held[cols:][:, None, :], jnp.zeros((), BF))
    mixed = dot(returned, table.reshape(experts * slots, frame_tokens), 0, 0).astype(BF)
    mixed = swap(mixed.reshape(cols, shards, tokens).transpose(1, 0, 2), "tok")
    mixed = mixed.reshape(width, tokens).astype(F32)
    layer_out = (residual.astype(F32) + shares[:, 3:4] * mixed).astype(BF)
    return layer_out.T[None]


def solution(mesh):
    return jax.shard_map(
        per_device,
        mesh=mesh,
        in_specs=(
            P("frame", "tok", None),
            P("frame", "tok", None),
            P("frame", "tok", None),
            P("frame", "tok", None),
            P("frame", None, None),
            P(),
            P(),
            P(),
            P("frame", None, "tok"),
            P("frame", "tok"),
            P("frame", "tok", None),
            P("frame", None),
            P(None, "frame"),
            P(None, "frame", None),
        ),
        out_specs=P("frame", "tok", None),
        check_vma=False,
    )
```

```python
import functools
import math

import jax
import jax.numpy as jnp
from jax import lax
from jax.experimental import pallas as pl
from jax.experimental.pallas import tpu as pltpu
from jax.sharding import PartitionSpec as P

H = 16
HD = 72
CAP = 256
BF = jnp.bfloat16
F32 = jnp.float32


def dot(a, b, ca, cb):
    return lax.dot_general(a, b, (((ca,), (cb,)), ((), ())), preferred_element_type=F32)


def attention_kernel(q_ref, k_ref, v_ref, o_ref):
    sources = q_ref.shape[0]
    scale = math.log2(math.e) / math.sqrt(HD)
    keys = jnp.concatenate([k_ref[s, 0] for s in range(sources)], axis=1).T
    values = jnp.concatenate([v_ref[s, 0] for s in range(sources)], axis=1)

    def block(j, carry):
        scores = dot(keys, q_ref[j, 0], 1, 0)
        top = jnp.max(scores, axis=0, keepdims=True)
        powers = jnp.exp2((scores - top) * scale)
        total = jnp.sum(powers, axis=0, keepdims=True)
        out = dot(values, powers.astype(BF), 1, 0)
        o_ref[j, 0] = (out / total).astype(BF)
        return carry

    lax.fori_loop(0, sources, block, 0)


def attention(q, k, v):
    sources, heads, _, tokens = q.shape
    spec = pl.BlockSpec((sources, 1, HD, tokens), lambda h: (0, h, 0, 0))
    return pl.pallas_call(
        attention_kernel,
        out_shape=jax.ShapeDtypeStruct(q.shape, BF),
        grid=(heads,),
        in_specs=[spec] * 3,
        out_specs=spec,
        compiler_params=pltpu.CompilerParams(vmem_limit_bytes=48 << 20),
    )(q, k, v)


def swap(x, axis):
    return lax.all_to_all(x, axis, split_axis=0, concat_axis=0, tiled=True)


MESH = pl.DeviceIdType.MESH


def gelu(x):
    return 0.5 * x * (1.0 + jnp.tanh(math.sqrt(2.0 / math.pi) * (x + 0.044715 * (x * x * x))))


def tail_kernel(
    att_ref,
    stream_ref,
    mod_ref,
    out_bias_ref,
    router_ref,
    expand_bias_ref,
    reduce_bias_ref,
    counts_ref,
    where_ref,
    wo_hbm,
    we_hbm,
    wr_hbm,
    o_ref,
    wo,
    we,
    wr,
    att_in,
    normed_out,
    normed_in,
    gate_out,
    gate_in,
    count_in,
    chosen_out,
    chosen_in,
    rows_all,
    part_out,
    part_in,
    ret_out,
    ret_in,
    mix_out,
    mix_in,
    local_sem,
    tok_send,
    tok_recv,
    frame_send,
    frame_recv,
):
    shards, cols, tokens = att_in.shape
    frames, slots = chosen_in.shape[0], chosen_in.shape[1]
    experts = gate_in.shape[1]
    frame_tokens = shards * tokens
    size = {"tok": shards, "frame": frames}
    me = {"tok": lax.axis_index("tok"), "frame": lax.axis_index("frame")}
    sems = {"tok": (tok_send, tok_recv), "frame": (frame_send, frame_recv)}

    loads = [
        pltpu.make_async_copy(src, dst, local_sem.at[i])
        for i, (src, dst) in enumerate(((wo_hbm, wo), (we_hbm, we), (wr_hbm, wr)))
    ]
    for load in loads:
        load.start()

    barrier = pltpu.get_barrier_semaphore()
    for axis in ("tok", "frame"):
        for d in range(1, size[axis]):
            p = lax.rem(me[axis] + d, size[axis])
            pl.semaphore_signal(barrier, inc=1, device_id={axis: p}, device_id_type=MESH)
    pl.semaphore_wait(barrier, shards + frames - 2)

    def copy(axis, phase, src, dst, to, slot):
        send, recv = sems[axis]
        return pltpu.make_async_remote_copy(
            src_ref=src,
            dst_ref=dst.at[slot],
            send_sem=send.at[phase, to],
            recv_sem=recv.at[phase, slot],
            device_id={axis: to},
            device_id_type=MESH,
        )

    sent = []

    def send_to(axis, phase, source, dst, d):
        p = lax.rem(me[axis] + d, size[axis])
        made = copy(axis, phase, source(p), dst, p, me[axis])
        made.start()
        sent.append(made)

    def send_all(axis, phase, source, dst):
        for d in range(1, size[axis]):
            send_to(axis, phase, source, dst, d)

    def take(axis, phase, source, dst, d):
        q = lax.rem(me[axis] + size[axis] - d, size[axis])
        copy(axis, phase, source(q), dst, q, q).wait_recv()
        return q

    def take_all(axis, phase, source, dst):
        for d in range(1, size[axis]):
            take(axis, phase, source, dst, d)

    tok, frame = me["tok"], me["frame"]
    send_all("tok", 0, lambda p: att_ref.at[p], att_in)
    send_all("frame", 0, lambda p: counts_ref.at[p], count_in)
    att_in[tok] = att_ref[tok]
    count_in[frame] = counts_ref[frame]
    loads[0].wait()
    take_all("tok", 0, lambda p: att_ref.at[p], att_in)

    projected = dot(att_in[0].T, wo[0:cols, :], 1, 0)
    for s in range(1, shards):
        projected += dot(att_in[s].T, wo[s * cols : (s + 1) * cols, :], 1, 0)
    projected += out_bias_ref[...]
    residual = (stream_ref[...].astype(F32) + mod_ref[0:1] * projected).astype(BF)
    wide = residual.astype(F32)
    centred = wide - jnp.mean(wide, axis=1, keepdims=True)
    variance = jnp.mean(centred * centred, axis=1, keepdims=True)
    normed = (
        centred * lax.rsqrt(variance + 1e-06) * (1.0 + mod_ref[2:3]) + mod_ref[1:2]
    ).astype(BF)
    turned = normed.T
    for s in range(shards):
        normed_out[s] = turned[s * cols : (s + 1) * cols]
    send_all("tok", 1, lambda p: normed_out.at[p], normed_in)
    o_ref[...] = residual
    gates = dot(router_ref[...], normed, 1, 1)
    gate_out[...] = 1.0 / (1.0 + jnp.exp(-gates))
    send_all("tok", 2, lambda p: gate_out, gate_in)
    normed_in[tok] = normed_out[tok]
    gate_in[tok] = gate_out[...]

    token = lax.broadcasted_iota(jnp.int32, (slots, frame_tokens), 1)

    def hits(e):
        return where_ref[e] == token

    take_all("frame", 0, lambda p: counts_ref.at[p], count_in)
    row = lax.broadcasted_iota(jnp.int32, (CAP, slots), 0)
    slot = lax.broadcasted_iota(jnp.int32, (CAP, slots), 1)
    first = jnp.zeros((1, slots), jnp.int32)
    firsts, numbers = [], []
    for g in range(frames):
        number = count_in[g][0:1, 0:slots]
        firsts.append(first)
        numbers.append(number)
        first = first + number

    def pack(g):
        return jnp.where((row == firsts[g] + slot) & (slot < numbers[g]), 1.0, 0.0)

    take_all("tok", 1, lambda p: normed_out.at[p], normed_in)
    held = jnp.concatenate([normed_in[s] for s in range(shards)], axis=1)
    for e in range(experts):
        pick = jnp.where(hits(e), 1.0, 0.0).astype(BF)
        chosen_out[e] = dot(pick, held, 1, 1).astype(BF)
    send_all("frame", 1, lambda p: chosen_out.at[p], chosen_in)
    chosen_in[frame] = chosen_out[frame]
    take_all("frame", 1, lambda p: chosen_out.at[p], chosen_in)
    rows = dot(pack(0).astype(BF), chosen_in[0], 1, 0)
    for g in range(1, frames):
        rows += dot(pack(g).astype(BF), chosen_in[g], 1, 0)
    rows_all[tok] = rows.astype(BF)
    send_all("tok", 3, lambda p: rows_all.at[tok], rows_all)
    loads[1].wait()
    loads[2].wait()
    take_all("tok", 3, lambda p: rows_all.at[tok], rows_all)
    hidden = dot(rows_all[0], we[0:cols, :], 1, 0)
    for s in range(1, shards):
        hidden += dot(rows_all[s], we[s * cols : (s + 1) * cols, :], 1, 0)
    hidden = gelu(hidden + expand_bias_ref[...]).astype(BF)
    partial_out = dot(hidden, wr[...], 1, 0)
    for s in range(shards):
        part_out[s] = partial_out[:, s * cols : (s + 1) * cols].astype(BF)
    send_all("tok", 4, lambda p: part_out.at[p], part_in)
    part_in[tok] = part_out[tok]
    take_all("tok", 4, lambda p: part_out.at[p], part_in)
    total = part_in[0].astype(F32)
    for s in range(1, shards):
        total += part_in[s].astype(F32)
    expert_out = (total + reduce_bias_ref[tok]).astype(BF)
    for g in range(frames):
        ret_out[g] = dot(pack(g).T.astype(BF), expert_out, 1, 0).astype(BF)
    send_all("frame", 2, lambda p: ret_out.at[p], ret_in)
    ret_in[frame] = ret_out[frame]
    take_all("tok", 2, lambda p: gate_out, gate_in)
    gate_all = jnp.concatenate([gate_in[s] for s in range(shards)], axis=1)
    take_all("frame", 2, lambda p: ret_out.at[p], ret_in)
    mixed = jnp.zeros((cols, frame_tokens), F32)
    for e in range(experts):
        table = jnp.where(hits(e), gate_all[e : e + 1], 0.0).astype(BF)
        mixed += dot(ret_in[e].T, table, 1, 0)
    for s in range(shards):
        mix_out[s] = mixed[:, s * tokens : (s + 1) * tokens].astype(BF)
    send_all("tok", 5, lambda p: mix_out.at[p], mix_in)
    mix_in[tok] = mix_out[tok]
    take_all("tok", 5, lambda p: mix_out.at[p], mix_in)
    mix = jnp.concatenate([mix_in[s].astype(F32) for s in range(shards)], axis=0).T
    o_ref[...] = (o_ref[...].astype(F32) + mod_ref[3:4] * mix).astype(BF)
    for made in sent:
        made.wait_send()


def per_device(
    stream,
    queries,
    key_vectors,
    value_vectors,
    modulation,
    output_weight,
    output_bias,
    router_weight,
    expand_weight,
    expand_bias,
    reduce_weight,
    reduce_bias,
    counts,
    picked_rows,
):
    shards = lax.axis_size("tok")
    frames = lax.axis_size("frame")
    tokens = stream.shape[1]
    width = stream.shape[2]
    hidden = expand_weight.shape[2]
    cols = width // shards
    heads = H // shards
    experts, _, slots = picked_rows.shape

    def to_heads(x):
        return swap(x[0].T.reshape(shards, heads, HD, tokens), "tok")

    attended = attention(to_heads(queries), to_heads(key_vectors), to_heads(value_vectors))
    attended = attended.reshape(shards, cols, tokens)
    used = jnp.arange(slots, dtype=jnp.int32)[None, :] < counts
    where_to = jnp.where(used, picked_rows[:, 0, :], -1)[:, :, None]
    vmem = pl.BlockSpec(memory_space=pltpu.VMEM)
    hbm = pl.BlockSpec(memory_space=pl.ANY)
    layer_out = pl.pallas_call(
        tail_kernel,
        out_shape=jax.ShapeDtypeStruct((tokens, width), BF),
        in_specs=[vmem] * 9 + [hbm] * 3,
        out_specs=vmem,
        scratch_shapes=[
            pltpu.VMEM((width, width), BF),
            pltpu.VMEM((width, hidden), BF),
            pltpu.VMEM((hidden, width), BF),
            pltpu.VMEM((shards, cols, tokens), BF),
            pltpu.VMEM((shards, cols, tokens), BF),
            pltpu.VMEM((shards, cols, tokens), BF),
            pltpu.VMEM((experts, tokens), F32),
            pltpu.VMEM((shards, experts, tokens), F32),
            pltpu.VMEM((frames, 8, 128), jnp.int32),
            pltpu.VMEM((frames, slots, cols), BF),
            pltpu.VMEM((frames, slots, cols), BF),
            pltpu.VMEM((shards, CAP, cols), BF),
            pltpu.VMEM((shards, CAP, cols), BF),
            pltpu.VMEM((shards, CAP, cols), BF),
            pltpu.VMEM((frames, slots, cols), BF),
            pltpu.VMEM((frames, slots, cols), BF),
            pltpu.VMEM((shards, cols, tokens), BF),
            pltpu.VMEM((shards, cols, tokens), BF),
            pltpu.SemaphoreType.DMA((3,)),
            pltpu.SemaphoreType.DMA((6, shards)),
            pltpu.SemaphoreType.DMA((6, shards)),
            pltpu.SemaphoreType.DMA((3, frames)),
            pltpu.SemaphoreType.DMA((3, frames)),
        ],
        compiler_params=pltpu.CompilerParams(
            collective_id=1, has_side_effects=True, vmem_limit_bytes=56 << 20
        ),
    )(
        attended,
        stream[0],
        modulation[0],
        output_bias[None],
        router_weight.T,
        expand_bias,
        reduce_bias.reshape(shards, 1, cols),
        jnp.broadcast_to(counts[:, :, None], (experts, 8, 128)),
        where_to,
        output_weight,
        expand_weight[0],
        reduce_weight[0],
    )
    return layer_out[None]


def solution(mesh):
    return jax.shard_map(
        per_device,
        mesh=mesh,
        in_specs=(
            P("frame", "tok", None),
            P("frame", "tok", None),
            P("frame", "tok", None),
            P("frame", "tok", None),
            P("frame", None, None),
            P(),
            P(),
            P(),
            P("frame", None, "tok"),
            P("frame", "tok"),
            P("frame", "tok", None),
            P("frame", None),
            P(None, "frame"),
            P(None, "frame", None),
        ),
        out_specs=P("frame", "tok", None),
        check_vma=False,
    )
```

```python
import math

import jax
import jax.numpy as jnp
from jax import lax
from jax.experimental import pallas as pl
from jax.experimental.pallas import tpu as pltpu
from jax.sharding import PartitionSpec as P

H = 16
HD = 72
CAP = 256
BF = jnp.bfloat16
F32 = jnp.float32


def dot(a, b, ca, cb):
    return lax.dot_general(a, b, (((ca,), (cb,)), ((), ())), preferred_element_type=F32)


MESH = pl.DeviceIdType.MESH


def gelu(x):
    return 0.5 * x * (1.0 + jnp.tanh(math.sqrt(2.0 / math.pi) * (x + 0.044715 * (x * x * x))))


def layer_kernel(
    q_ref,
    k_ref,
    v_ref,
    stream_ref,
    mod_ref,
    out_bias_ref,
    router_ref,
    expand_bias_ref,
    reduce_bias_ref,
    counts_ref,
    where_ref,
    wo_hbm,
    we_hbm,
    wr_hbm,
    o_ref,
    wo,
    we,
    wr,
    qkv_out,
    qkv_in,
    att_out,
    att_in,
    picks,
    packs,
    packs_turned,
    normed_out,
    normed_in,
    gate_out,
    gate_in,
    count_in,
    chosen_out,
    chosen_in,
    rows_all,
    part_out,
    part_in,
    ret_out,
    ret_in,
    mix_out,
    mix_in,
    local_sem,
    head_send,
    head_recv,
    tok_send,
    tok_recv,
    frame_send,
    frame_recv,
):
    shards, heads, _, tokens = att_in.shape
    cols = heads * HD
    frames, slots = chosen_in.shape[0], chosen_in.shape[1]
    experts = gate_in.shape[1]
    frame_tokens = shards * tokens
    size = {"tok": shards, "frame": frames}
    me = {"tok": lax.axis_index("tok"), "frame": lax.axis_index("frame")}
    sems = {
        "tok": (tok_send, tok_recv),
        "frame": (frame_send, frame_recv),
        "head": (head_send, head_recv),
    }
    size["head"], me["head"] = size["tok"], me["tok"]
    real = {"tok": "tok", "frame": "frame", "head": "tok"}

    loads = [
        pltpu.make_async_copy(src, dst, local_sem.at[i])
        for i, (src, dst) in enumerate(((wo_hbm, wo), (we_hbm, we), (wr_hbm, wr)))
    ]
    for load in loads:
        load.start()

    barrier = pltpu.get_barrier_semaphore()
    for axis in ("tok", "frame"):
        for d in range(1, size[axis]):
            p = lax.rem(me[axis] + d, size[axis])
            pl.semaphore_signal(barrier, inc=1, device_id={axis: p}, device_id_type=MESH)
    pl.semaphore_wait(barrier, shards + frames - 2)

    def copy(axis, phase, src, dst, to, slot):
        send, recv = sems[axis]
        return pltpu.make_async_remote_copy(
            src_ref=src,
            dst_ref=dst.at[slot],
            send_sem=send.at[phase, to],
            recv_sem=recv.at[phase, slot],
            device_id={real[axis]: to},
            device_id_type=MESH,
        )

    sent = []

    def send_to(axis, phase, source, dst, d):
        p = lax.rem(me[axis] + d, size[axis])
        made = copy(axis, phase, source(p), dst, p, me[axis])
        made.start()
        sent.append(made)

    def send_all(axis, phase, source, dst):
        for d in range(1, size[axis]):
            send_to(axis, phase, source, dst, d)

    def take(axis, phase, source, dst, d):
        q = lax.rem(me[axis] + size[axis] - d, size[axis])
        copy(axis, phase, source(q), dst, q, q).wait_recv()
        return q

    def take_all(axis, phase, source, dst):
        for d in range(1, size[axis]):
            take(axis, phase, source, dst, d)

    tok, frame = me["tok"], me["frame"]
    send_all("frame", 0, lambda p: counts_ref.at[p], count_in)
    count_in[frame] = counts_ref[frame]

    def part(t, h):
        return (t * heads + h, lambda p: qkv_out.at[t, p, h], qkv_in.at[t, :, h])

    for t, ref in enumerate((k_ref, q_ref, v_ref)):
        turned = ref[...].astype(F32).T
        for h in range(heads):
            for s in range(shards):
                base = s * cols + h * HD
                qkv_out[t, s, h] = turned[base : base + HD].astype(BF)
            if h == 0:
                send_all("head", *part(t, h))
    for h in range(1, heads):
        for t in range(3):
            send_all("head", *part(t, h))
    for t in range(3):
        qkv_in[t, tok] = qkv_out[t, tok]

    token = lax.broadcasted_iota(jnp.int32, (slots, frame_tokens), 1)
    for e in range(experts):
        picks[e] = jnp.where(where_ref[e] == token, 1.0, 0.0).astype(BF)

    scale = math.log2(math.e) / math.sqrt(HD)
    for h in range(heads):
        for t in range(3):
            take_all("head", *part(t, h))
        keys = jnp.concatenate([qkv_in[0, s, h] for s in range(shards)], axis=1).T
        values = jnp.concatenate([qkv_in[2, s, h] for s in range(shards)], axis=1)

        def block(j, carry):
            scores = dot(keys, qkv_in[1, j, h], 1, 0)
            top = jnp.max(scores, axis=0, keepdims=True)
            powers = jnp.exp2((scores - top) * scale)
            denominator = jnp.sum(powers, axis=0, keepdims=True)
            out = dot(values, powers.astype(BF), 1, 0)
            att_out[j, h] = (out / denominator).astype(BF)
            return carry

        lax.fori_loop(0, shards, block, 0)
        send_all("head", 3 * heads + h, lambda p: att_out.at[p, h], att_in.at[:, h])
        att_in[tok, h] = att_out[tok, h]

    take_all("frame", 0, lambda p: counts_ref.at[p], count_in)
    row = lax.broadcasted_iota(jnp.int32, (CAP, slots), 0)
    slot = lax.broadcasted_iota(jnp.int32, (CAP, slots), 1)
    first = jnp.zeros((1, slots), jnp.int32)
    for g in range(frames):
        number = count_in[g][0:1, 0:slots]
        pack = jnp.where((row == first + slot) & (slot < number), 1.0, 0.0)
        packs[g] = pack.astype(BF)
        packs_turned[g] = pack.T.astype(BF)
        first = first + number
    loads[0].wait()

    def project(q):
        block = jnp.concatenate([att_in[q, h].astype(F32) for h in range(heads)], axis=0)
        return dot(block.T.astype(BF), wo[q], 1, 0)

    projected = project(tok)
    for d in range(1, shards):
        for h in range(heads):
            q = take("head", 3 * heads + h, lambda p: att_out.at[p, h], att_in.at[:, h], d)
        projected += project(q)
    projected += out_bias_ref[...]
    residual = (stream_ref[...].astype(F32) + mod_ref[0:1] * projected).astype(BF)
    wide = residual.astype(F32)
    centred = wide - jnp.mean(wide, axis=1, keepdims=True)
    variance = jnp.mean(centred * centred, axis=1, keepdims=True)
    normed = (
        centred * lax.rsqrt(variance + 1e-06) * (1.0 + mod_ref[2:3]) + mod_ref[1:2]
    ).astype(BF)
    turned = normed.T
    for s in range(shards):
        normed_out[s] = turned[s * cols : (s + 1) * cols]
    send_all("tok", 1, lambda p: normed_out.at[p], normed_in)
    o_ref[...] = residual
    gates = dot(router_ref[...], normed, 1, 1)
    gate_out[...] = 1.0 / (1.0 + jnp.exp(-gates))
    send_all("tok", 2, lambda p: gate_out, gate_in)
    normed_in[tok] = normed_out[tok]
    gate_in[tok] = gate_out[...]

    take_all("tok", 1, lambda p: normed_out.at[p], normed_in)
    held = jnp.concatenate([normed_in[s] for s in range(shards)], axis=1)
    for d in range(1, frames + 1):
        p = lax.rem(frame + d, frames)
        chosen_out[p] = dot(picks[p], held, 1, 1).astype(BF)
        if d < frames:
            send_to("frame", 1, lambda p: chosen_out.at[p], chosen_in, d)
    rows = dot(packs[frame], chosen_out[frame], 1, 0)
    for d in range(1, frames):
        g = take("frame", 1, lambda p: chosen_out.at[p], chosen_in, d)
        rows += dot(packs[g], chosen_in[g], 1, 0)
    rows_all[tok] = rows.astype(BF)
    send_all("tok", 3, lambda p: rows_all.at[tok], rows_all)
    loads[1].wait()
    loads[2].wait()
    hidden = dot(rows_all[tok], we[tok], 1, 0)
    for d in range(1, shards):
        q = take("tok", 3, lambda p: rows_all.at[tok], rows_all, d)
        hidden += dot(rows_all[q], we[q], 1, 0)
    hidden = gelu(hidden + expand_bias_ref[...]).astype(BF)
    partial_out = dot(hidden, wr[...], 1, 0)
    for s in range(shards):
        part_out[s] = partial_out[:, s * cols : (s + 1) * cols].astype(BF)
    send_all("tok", 4, lambda p: part_out.at[p], part_in)
    part_in[tok] = part_out[tok]
    take_all("tok", 4, lambda p: part_out.at[p], part_in)
    total = part_in[0].astype(F32)
    for s in range(1, shards):
        total += part_in[s].astype(F32)
    expert_out = (total + reduce_bias_ref[tok]).astype(BF)
    for d in range(1, frames + 1):
        p = lax.rem(frame + d, frames)
        ret_out[p] = dot(packs_turned[p], expert_out, 1, 0).astype(BF)
        if d < frames:
            send_to("frame", 2, lambda p: ret_out.at[p], ret_in, d)
    take_all("tok", 2, lambda p: gate_out, gate_in)
    gate_all = jnp.concatenate([gate_in[s] for s in range(shards)], axis=1).astype(BF)
    for e in range(experts):
        picks[e] = picks[e] * gate_all[e : e + 1]
    mixed = dot(ret_out[frame].T, picks[frame], 1, 0)
    for d in range(1, frames):
        e = take("frame", 2, lambda p: ret_out.at[p], ret_in, d)
        mixed += dot(ret_in[e].T, picks[e], 1, 0)
    for s in range(shards):
        mix_out[s] = mixed[:, s * tokens : (s + 1) * tokens].astype(BF)
    send_all("tok", 5, lambda p: mix_out.at[p], mix_in)
    mix_in[tok] = mix_out[tok]
    take_all("tok", 5, lambda p: mix_out.at[p], mix_in)
    mix = jnp.concatenate([mix_in[s].astype(F32) for s in range(shards)], axis=0).T
    o_ref[...] = (o_ref[...].astype(F32) + mod_ref[3:4] * mix).astype(BF)
    for made in sent:
        made.wait_send()


def per_device(
    stream,
    queries,
    key_vectors,
    value_vectors,
    modulation,
    output_weight,
    output_bias,
    router_weight,
    expand_weight,
    expand_bias,
    reduce_weight,
    reduce_bias,
    counts,
    picked_rows,
):
    shards = lax.axis_size("tok")
    frames = lax.axis_size("frame")
    tokens = stream.shape[1]
    width = stream.shape[2]
    hidden = expand_weight.shape[2]
    cols = width // shards
    heads = H // shards
    experts, _, slots = picked_rows.shape

    used = jnp.arange(slots, dtype=jnp.int32)[None, :] < counts
    where_to = jnp.where(used, picked_rows[:, 0, :], -1)[:, :, None]
    vmem = pl.BlockSpec(memory_space=pltpu.VMEM)
    hbm = pl.BlockSpec(memory_space=pl.ANY)
    layer_out = pl.pallas_call(
        layer_kernel,
        out_shape=jax.ShapeDtypeStruct((tokens, width), BF),
        in_specs=[vmem] * 11 + [hbm] * 3,
        out_specs=vmem,
        scratch_shapes=[
            pltpu.VMEM((shards, cols, width), BF),
            pltpu.VMEM((shards, cols, hidden), BF),
            pltpu.VMEM((hidden, width), BF),
            pltpu.VMEM((3, shards, heads, HD, tokens), BF),
            pltpu.VMEM((3, shards, heads, HD, tokens), BF),
            pltpu.VMEM((shards, heads, HD, tokens), BF),
            pltpu.VMEM((shards, heads, HD, tokens), BF),
            pltpu.VMEM((experts, slots, shards * tokens), BF),
            pltpu.VMEM((frames, CAP, slots), BF),
            pltpu.VMEM((frames, slots, CAP), BF),
            pltpu.VMEM((shards, cols, tokens), BF),
            pltpu.VMEM((shards, cols, tokens), BF),
            pltpu.VMEM((experts, tokens), F32),
            pltpu.VMEM((shards, experts, tokens), F32),
            pltpu.VMEM((frames, 8, 128), jnp.int32),
            pltpu.VMEM((frames, slots, cols), BF),
            pltpu.VMEM((frames, slots, cols), BF),
            pltpu.VMEM((shards, CAP, cols), BF),
            pltpu.VMEM((shards, CAP, cols), BF),
            pltpu.VMEM((shards, CAP, cols), BF),
            pltpu.VMEM((frames, slots, cols), BF),
            pltpu.VMEM((frames, slots, cols), BF),
            pltpu.VMEM((shards, cols, tokens), BF),
            pltpu.VMEM((shards, cols, tokens), BF),
            pltpu.SemaphoreType.DMA((3,)),
            pltpu.SemaphoreType.DMA((4 * heads, shards)),
            pltpu.SemaphoreType.DMA((4 * heads, shards)),
            pltpu.SemaphoreType.DMA((6, shards)),
            pltpu.SemaphoreType.DMA((6, shards)),
            pltpu.SemaphoreType.DMA((3, frames)),
            pltpu.SemaphoreType.DMA((3, frames)),
        ],
        compiler_params=pltpu.CompilerParams(
            collective_id=1, has_side_effects=True, vmem_limit_bytes=56 << 20
        ),
    )(
        queries[0],
        key_vectors[0],
        value_vectors[0],
        stream[0],
        modulation[0],
        output_bias[None],
        router_weight.T,
        expand_bias,
        reduce_bias.reshape(shards, 1, cols),
        jnp.broadcast_to(counts[:, :, None], (experts, 8, 128)),
        where_to,
        output_weight.reshape(shards, cols, width),
        expand_weight[0].reshape(shards, cols, hidden),
        reduce_weight[0],
    )
    return layer_out[None]


def solution(mesh):
    return jax.shard_map(
        per_device,
        mesh=mesh,
        in_specs=(
            P("frame", "tok", None),
            P("frame", "tok", None),
            P("frame", "tok", None),
            P("frame", "tok", None),
            P("frame", None, None),
            P(),
            P(),
            P(),
            P("frame", None, "tok"),
            P("frame", "tok"),
            P("frame", "tok", None),
            P("frame", None),
            P(None, "frame"),
            P(None, "frame", None),
        ),
        out_specs=P("frame", "tok", None),
        check_vma=False,
    )
```

```python
import math

import jax
import jax.numpy as jnp
from jax import lax
from jax.experimental import pallas as pl
from jax.experimental.pallas import tpu as pltpu
from jax.sharding import PartitionSpec as P

H = 16
HD = 72
CAP = 256
BF = jnp.bfloat16
F32 = jnp.float32


def dot(a, b, ca, cb):
    return lax.dot_general(a, b, (((ca,), (cb,)), ((), ())), preferred_element_type=F32)


MESH = pl.DeviceIdType.MESH


def gelu(x):
    return 0.5 * x * (1.0 + jnp.tanh(math.sqrt(2.0 / math.pi) * (x + 0.044715 * (x * x * x))))


def packed_shape(slots, cols):
    full, rest = cols // 128, cols % 128
    if full and rest and 128 % rest == 0 and slots % (128 // rest) == 0:
        if slots * rest // 128 % 8 == 0 and slots % 16 == 0:
            return (full * slots + slots * rest // 128, 128)
    return (slots, cols)


def put_block(ref, at, x, slots):
    cols = x.shape[1]
    if ref.shape[1:] == (slots, cols):
        ref[at] = x.astype(BF)
        return
    full, rest = cols // 128, cols % 128
    for i in range(full):
        ref[at, i * slots : (i + 1) * slots, :] = x[:, i * 128 : (i + 1) * 128].astype(BF)
    high = slots * rest // 128
    tail = [x[i * high : (i + 1) * high, full * 128 :] for i in range(128 // rest)]
    ref[at, full * slots : full * slots + high, :] = jnp.concatenate(tail, axis=1).astype(BF)


def get_block(ref, at, slots, cols):
    if ref.shape[1:] == (slots, cols):
        return ref[at]
    full, rest = cols // 128, cols % 128
    high = slots * rest // 128
    parts = [ref[at, i * slots : (i + 1) * slots, :] for i in range(full)]
    tail = ref[at, full * slots : full * slots + high, :].astype(F32)
    tail = [tail[:, i * rest : (i + 1) * rest] for i in range(128 // rest)]
    return jnp.concatenate(parts + [jnp.concatenate(tail, axis=0).astype(BF)], axis=1)


def layer_kernel(
    q_ref,
    k_ref,
    v_ref,
    stream_ref,
    mod_ref,
    out_bias_ref,
    router_ref,
    expand_bias_ref,
    reduce_bias_ref,
    counts_ref,
    where_ref,
    wo_hbm,
    we_hbm,
    wr_hbm,
    o_ref,
    wo,
    we,
    wr,
    qkv_out,
    qkv_in,
    att_out,
    att_in,
    picks,
    packs,
    packs_turned,
    normed_out,
    normed_in,
    gate_out,
    gate_in,
    count_in,
    chosen_out,
    chosen_in,
    rows_all,
    part_out,
    part_in,
    ret_out,
    ret_in,
    mix_out,
    mix_in,
    local_sem,
    head_send,
    head_recv,
    tok_send,
    tok_recv,
    frame_send,
    frame_recv,
):
    shards, heads, _, tokens = att_in.shape
    cols = heads * HD
    frames, slots = packs.shape[0], packs.shape[2]
    experts = gate_in.shape[1]
    frame_tokens = shards * tokens
    size = {"tok": shards, "frame": frames}
    me = {"tok": lax.axis_index("tok"), "frame": lax.axis_index("frame")}
    sems = {
        "tok": (tok_send, tok_recv),
        "frame": (frame_send, frame_recv),
        "head": (head_send, head_recv),
    }
    size["head"], me["head"] = size["tok"], me["tok"]
    real = {"tok": "tok", "frame": "frame", "head": "tok"}

    loads = [
        pltpu.make_async_copy(src, dst, local_sem.at[i])
        for i, (src, dst) in enumerate(((wo_hbm, wo), (we_hbm, we), (wr_hbm, wr)))
    ]
    for load in loads:
        load.start()

    barrier = pltpu.get_barrier_semaphore()
    for axis in ("tok", "frame"):
        for d in range(1, size[axis]):
            p = lax.rem(me[axis] + d, size[axis])
            pl.semaphore_signal(barrier, inc=1, device_id={axis: p}, device_id_type=MESH)
    pl.semaphore_wait(barrier, shards + frames - 2)

    def copy(axis, phase, src, dst, to, slot):
        send, recv = sems[axis]
        return pltpu.make_async_remote_copy(
            src_ref=src,
            dst_ref=dst.at[slot],
            send_sem=send.at[phase, to],
            recv_sem=recv.at[phase, slot],
            device_id={real[axis]: to},
            device_id_type=MESH,
        )

    sent = []

    def send_to(axis, phase, source, dst, d):
        p = lax.rem(me[axis] + d, size[axis])
        made = copy(axis, phase, source(p), dst, p, me[axis])
        made.start()
        sent.append(made)

    def send_all(axis, phase, source, dst):
        for d in range(1, size[axis]):
            send_to(axis, phase, source, dst, d)

    def take(axis, phase, source, dst, d):
        q = lax.rem(me[axis] + size[axis] - d, size[axis])
        copy(axis, phase, source(q), dst, q, q).wait_recv()
        return q

    def take_all(axis, phase, source, dst):
        for d in range(1, size[axis]):
            take(axis, phase, source, dst, d)

    tok, frame = me["tok"], me["frame"]
    send_all("frame", 0, lambda p: counts_ref.at[p], count_in)
    count_in[frame] = counts_ref[frame]

    def part(t, h):
        return (t * heads + h, lambda p: qkv_out.at[t, p, h], qkv_in.at[t, :, h])

    for t, ref in enumerate((k_ref, q_ref, v_ref)):
        turned = ref[...].astype(F32).T
        for h in range(heads):
            for s in range(shards):
                base = s * cols + h * HD
                qkv_out[t, s, h] = turned[base : base + HD].astype(BF)
            if h == 0:
                send_all("head", *part(t, h))
    for h in range(1, heads):
        for t in range(3):
            send_all("head", *part(t, h))
    for t in range(3):
        qkv_in[t, tok] = qkv_out[t, tok]

    token = lax.broadcasted_iota(jnp.int32, (slots, frame_tokens), 1)
    for e in range(experts):
        picks[e] = jnp.where(where_ref[e] == token, 1.0, 0.0).astype(BF)

    scale = math.log2(math.e) / math.sqrt(HD)
    for h in range(heads):
        for t in range(3):
            take_all("head", *part(t, h))
        keys = jnp.concatenate([qkv_in[0, s, h] for s in range(shards)], axis=1).T
        values = jnp.concatenate([qkv_in[2, s, h] for s in range(shards)], axis=1)

        def block(j, carry):
            scores = dot(keys, qkv_in[1, j, h], 1, 0)
            top = jnp.max(scores, axis=0, keepdims=True)
            powers = jnp.exp2((scores - top) * scale)
            denominator = jnp.sum(powers, axis=0, keepdims=True)
            out = dot(values, powers.astype(BF), 1, 0)
            att_out[j, h] = (out / denominator).astype(BF)
            return carry

        lax.fori_loop(0, shards, block, 0)
        send_all("head", 3 * heads + h, lambda p: att_out.at[p, h], att_in.at[:, h])
        att_in[tok, h] = att_out[tok, h]

    take_all("frame", 0, lambda p: counts_ref.at[p], count_in)
    row = lax.broadcasted_iota(jnp.int32, (CAP, slots), 0)
    slot = lax.broadcasted_iota(jnp.int32, (CAP, slots), 1)
    first = jnp.zeros((1, slots), jnp.int32)
    for g in range(frames):
        number = count_in[g][0:1, 0:slots]
        pack = jnp.where((row == first + slot) & (slot < number), 1.0, 0.0)
        packs[g] = pack.astype(BF)
        packs_turned[g] = pack.T.astype(BF)
        first = first + number
    loads[0].wait()

    def project(q):
        block = jnp.concatenate([att_in[q, h].astype(F32) for h in range(heads)], axis=0)
        return dot(block.T.astype(BF), wo[q], 1, 0)

    projected = project(tok)
    for d in range(1, shards):
        for h in range(heads):
            q = take("head", 3 * heads + h, lambda p: att_out.at[p, h], att_in.at[:, h], d)
        projected += project(q)
    projected += out_bias_ref[...]
    residual = (stream_ref[...].astype(F32) + mod_ref[0:1] * projected).astype(BF)
    wide = residual.astype(F32)
    centred = wide - jnp.mean(wide, axis=1, keepdims=True)
    variance = jnp.mean(centred * centred, axis=1, keepdims=True)
    normed = (
        centred * lax.rsqrt(variance + 1e-06) * (1.0 + mod_ref[2:3]) + mod_ref[1:2]
    ).astype(BF)
    turned = normed.T
    for s in range(shards):
        normed_out[s] = turned[s * cols : (s + 1) * cols]
    send_all("tok", 1, lambda p: normed_out.at[p], normed_in)
    o_ref[...] = residual
    gates = dot(router_ref[...], normed, 1, 1)
    gate_out[...] = 1.0 / (1.0 + jnp.exp(-gates))
    send_all("tok", 2, lambda p: gate_out, gate_in)
    normed_in[tok] = normed_out[tok]
    gate_in[tok] = gate_out[...]

    take_all("tok", 1, lambda p: normed_out.at[p], normed_in)
    held = jnp.concatenate([normed_in[s] for s in range(shards)], axis=1)
    for d in range(1, frames + 1):
        p = lax.rem(frame + d, frames)
        put_block(chosen_out, p, dot(picks[p], held, 1, 1), slots)
        if d < frames:
            send_to("frame", 1, lambda p: chosen_out.at[p], chosen_in, d)
    rows = dot(packs[frame], get_block(chosen_out, frame, slots, cols), 1, 0)
    for d in range(1, frames):
        g = take("frame", 1, lambda p: chosen_out.at[p], chosen_in, d)
        rows += dot(packs[g], get_block(chosen_in, g, slots, cols), 1, 0)
    rows_all[tok] = rows.T.astype(BF)
    send_all("tok", 3, lambda p: rows_all.at[tok], rows_all)
    loads[1].wait()
    loads[2].wait()
    hidden = dot(rows_all[tok].T, we[tok], 1, 0)
    for d in range(1, shards):
        q = take("tok", 3, lambda p: rows_all.at[tok], rows_all, d)
        hidden += dot(rows_all[q].T, we[q], 1, 0)
    hidden = gelu(hidden + expand_bias_ref[...]).astype(BF)
    partial_out = dot(hidden, wr[...], 1, 0).T
    for s in range(shards):
        part_out[s] = partial_out[s * cols : (s + 1) * cols].astype(BF)
    send_all("tok", 4, lambda p: part_out.at[p], part_in)
    part_in[tok] = part_out[tok]
    take_all("tok", 4, lambda p: part_out.at[p], part_in)
    total = part_in[0].astype(F32)
    for s in range(1, shards):
        total += part_in[s].astype(F32)
    expert_out = (total + reduce_bias_ref[tok]).astype(BF)
    for d in range(1, frames + 1):
        p = lax.rem(frame + d, frames)
        put_block(ret_out, p, dot(packs_turned[p], expert_out, 1, 1), slots)
        if d < frames:
            send_to("frame", 2, lambda p: ret_out.at[p], ret_in, d)
    take_all("tok", 2, lambda p: gate_out, gate_in)
    gate_all = jnp.concatenate([gate_in[s] for s in range(shards)], axis=1).astype(BF)
    for e in range(experts):
        picks[e] = picks[e] * gate_all[e : e + 1]
    mixed = dot(get_block(ret_out, frame, slots, cols).T, picks[frame], 1, 0)
    for d in range(1, frames):
        e = take("frame", 2, lambda p: ret_out.at[p], ret_in, d)
        mixed += dot(get_block(ret_in, e, slots, cols).T, picks[e], 1, 0)
    for s in range(shards):
        mix_out[s] = mixed[:, s * tokens : (s + 1) * tokens].astype(BF)
    send_all("tok", 5, lambda p: mix_out.at[p], mix_in)
    mix_in[tok] = mix_out[tok]
    take_all("tok", 5, lambda p: mix_out.at[p], mix_in)
    mix = jnp.concatenate([mix_in[s].astype(F32) for s in range(shards)], axis=0).T
    o_ref[...] = (o_ref[...].astype(F32) + mod_ref[3:4] * mix).astype(BF)
    for made in sent:
        made.wait_send()


def per_device(
    stream,
    queries,
    key_vectors,
    value_vectors,
    modulation,
    output_weight,
    output_bias,
    router_weight,
    expand_weight,
    expand_bias,
    reduce_weight,
    reduce_bias,
    counts,
    picked_rows,
):
    shards = lax.axis_size("tok")
    frames = lax.axis_size("frame")
    tokens = stream.shape[1]
    width = stream.shape[2]
    hidden = expand_weight.shape[2]
    cols = width // shards
    heads = H // shards
    experts, _, slots = picked_rows.shape

    used = jnp.arange(slots, dtype=jnp.int32)[None, :] < counts
    where_to = jnp.where(used, picked_rows[:, 0, :], -1)[:, :, None]
    vmem = pl.BlockSpec(memory_space=pltpu.VMEM)
    hbm = pl.BlockSpec(memory_space=pl.ANY)
    layer_out = pl.pallas_call(
        layer_kernel,
        out_shape=jax.ShapeDtypeStruct((tokens, width), BF),
        in_specs=[vmem] * 11 + [hbm] * 3,
        out_specs=vmem,
        scratch_shapes=[
            pltpu.VMEM((shards, cols, width), BF),
            pltpu.VMEM((shards, cols, hidden), BF),
            pltpu.VMEM((hidden, width), BF),
            pltpu.VMEM((3, shards, heads, HD, tokens), BF),
            pltpu.VMEM((3, shards, heads, HD, tokens), BF),
            pltpu.VMEM((shards, heads, HD, tokens), BF),
            pltpu.VMEM((shards, heads, HD, tokens), BF),
            pltpu.VMEM((experts, slots, shards * tokens), BF),
            pltpu.VMEM((frames, CAP, slots), BF),
            pltpu.VMEM((frames, slots, CAP), BF),
            pltpu.VMEM((shards, cols, tokens), BF),
            pltpu.VMEM((shards, cols, tokens), BF),
            pltpu.VMEM((experts, tokens), F32),
            pltpu.VMEM((shards, experts, tokens), F32),
            pltpu.VMEM((frames, 8, 128), jnp.int32),
            pltpu.VMEM((frames, *packed_shape(slots, cols)), BF),
            pltpu.VMEM((frames, *packed_shape(slots, cols)), BF),
            pltpu.VMEM((shards, cols, CAP), BF),
            pltpu.VMEM((shards, cols, CAP), BF),
            pltpu.VMEM((shards, cols, CAP), BF),
            pltpu.VMEM((frames, *packed_shape(slots, cols)), BF),
            pltpu.VMEM((frames, *packed_shape(slots, cols)), BF),
            pltpu.VMEM((shards, cols, tokens), BF),
            pltpu.VMEM((shards, cols, tokens), BF),
            pltpu.SemaphoreType.DMA((3,)),
            pltpu.SemaphoreType.DMA((4 * heads, shards)),
            pltpu.SemaphoreType.DMA((4 * heads, shards)),
            pltpu.SemaphoreType.DMA((6, shards)),
            pltpu.SemaphoreType.DMA((6, shards)),
            pltpu.SemaphoreType.DMA((3, frames)),
            pltpu.SemaphoreType.DMA((3, frames)),
        ],
        compiler_params=pltpu.CompilerParams(
            collective_id=1, has_side_effects=True, vmem_limit_bytes=56 << 20
        ),
    )(
        queries[0],
        key_vectors[0],
        value_vectors[0],
        stream[0],
        modulation[0],
        output_bias[None],
        router_weight.T,
        expand_bias,
        reduce_bias.reshape(shards, cols, 1),
        jnp.broadcast_to(counts[:, :, None], (experts, 8, 128)),
        where_to,
        output_weight.reshape(shards, cols, width),
        expand_weight[0].reshape(shards, cols, hidden),
        reduce_weight[0],
    )
    return layer_out[None]


def solution(mesh):
    return jax.shard_map(
        per_device,
        mesh=mesh,
        in_specs=(
            P("frame", "tok", None),
            P("frame", "tok", None),
            P("frame", "tok", None),
            P("frame", "tok", None),
            P("frame", None, None),
            P(),
            P(),
            P(),
            P("frame", None, "tok"),
            P("frame", "tok"),
            P("frame", "tok", None),
            P("frame", None),
            P(None, "frame"),
            P(None, "frame", None),
        ),
        out_specs=P("frame", "tok", None),
        check_vma=False,
    )
```

```python
import math

import jax
import jax.numpy as jnp
from jax import lax
from jax.experimental import pallas as pl
from jax.experimental.pallas import tpu as pltpu
from jax.sharding import PartitionSpec as P

H = 16
HD = 72
CAP = 256
BF = jnp.bfloat16
F32 = jnp.float32


def dot(a, b, ca, cb):
    return lax.dot_general(a, b, (((ca,), (cb,)), ((), ())), preferred_element_type=F32)


MESH = pl.DeviceIdType.MESH


def gelu(x):
    return 0.5 * x * (1.0 + jnp.tanh(math.sqrt(2.0 / math.pi) * (x + 0.044715 * (x * x * x))))


def packed_shape(slots, cols):
    full, rest = cols // 128, cols % 128
    if full and rest and 128 % rest == 0 and slots % (128 // rest) == 0:
        if slots * rest // 128 % 8 == 0 and slots % 16 == 0:
            return (full * slots + slots * rest // 128, 128)
    return (slots, cols)


def put_block(ref, at, x, slots):
    cols = x.shape[1]
    if ref.shape[1:] == (slots, cols):
        ref[at] = x.astype(BF)
        return
    full, rest = cols // 128, cols % 128
    for i in range(full):
        ref[at, i * slots : (i + 1) * slots, :] = x[:, i * 128 : (i + 1) * 128].astype(BF)
    high = slots * rest // 128
    tail = [x[i * high : (i + 1) * high, full * 128 :] for i in range(128 // rest)]
    ref[at, full * slots : full * slots + high, :] = jnp.concatenate(tail, axis=1).astype(BF)


def get_block(ref, at, slots, cols):
    if ref.shape[1:] == (slots, cols):
        return ref[at]
    full, rest = cols // 128, cols % 128
    high = slots * rest // 128
    parts = [ref[at, i * slots : (i + 1) * slots, :] for i in range(full)]
    tail = ref[at, full * slots : full * slots + high, :].astype(F32)
    tail = [tail[:, i * rest : (i + 1) * rest] for i in range(128 // rest)]
    return jnp.concatenate(parts + [jnp.concatenate(tail, axis=0).astype(BF)], axis=1)


def layer_kernel(
    q_ref,
    k_ref,
    v_ref,
    stream_ref,
    mod_ref,
    out_bias_ref,
    router_ref,
    expand_bias_ref,
    reduce_bias_row,
    own_counts_ref,
    picked_ref,
    wo_hbm,
    we_hbm,
    wr_hbm,
    o_ref,
    wo,
    we,
    wr,
    qkv_out,
    qkv_in,
    att_out,
    att_in,
    picks,
    packs,
    packs_turned,
    normed_out,
    normed_in,
    gate_out,
    gate_in,
    reduce_bias_ref,
    counts_ref,
    count_in,
    chosen_out,
    chosen_in,
    rows_all,
    part_out,
    part_in,
    ret_out,
    ret_in,
    mix_out,
    mix_in,
    local_sem,
    head_send,
    head_recv,
    tok_send,
    tok_recv,
    frame_send,
    frame_recv,
):
    shards, heads, _, tokens = att_in.shape
    cols = heads * HD
    frames, slots = packs.shape[0], packs.shape[2]
    experts = gate_in.shape[1]
    frame_tokens = shards * tokens
    size = {"tok": shards, "frame": frames}
    me = {"tok": lax.axis_index("tok"), "frame": lax.axis_index("frame")}
    sems = {
        "tok": (tok_send, tok_recv),
        "frame": (frame_send, frame_recv),
        "head": (head_send, head_recv),
    }
    size["head"], me["head"] = size["tok"], me["tok"]
    real = {"tok": "tok", "frame": "frame", "head": "tok"}

    loads = [
        pltpu.make_async_copy(src, dst, local_sem.at[i])
        for i, (src, dst) in enumerate(((wo_hbm, wo), (we_hbm, we), (wr_hbm, wr)))
    ]
    for load in loads:
        load.start()

    barrier = pltpu.get_barrier_semaphore()
    for axis in ("tok", "frame"):
        for d in range(1, size[axis]):
            p = lax.rem(me[axis] + d, size[axis])
            pl.semaphore_signal(barrier, inc=1, device_id={axis: p}, device_id_type=MESH)
    pl.semaphore_wait(barrier, shards + frames - 2)

    def copy(axis, phase, src, dst, to, slot):
        send, recv = sems[axis]
        return pltpu.make_async_remote_copy(
            src_ref=src,
            dst_ref=dst.at[slot],
            send_sem=send.at[phase, to],
            recv_sem=recv.at[phase, slot],
            device_id={real[axis]: to},
            device_id_type=MESH,
        )

    sent = []

    def send_to(axis, phase, source, dst, d):
        p = lax.rem(me[axis] + d, size[axis])
        made = copy(axis, phase, source(p), dst, p, me[axis])
        made.start()
        sent.append(made)

    def send_all(axis, phase, source, dst):
        for d in range(1, size[axis]):
            send_to(axis, phase, source, dst, d)

    def take(axis, phase, source, dst, d):
        q = lax.rem(me[axis] + size[axis] - d, size[axis])
        copy(axis, phase, source(q), dst, q, q).wait_recv()
        return q

    def take_all(axis, phase, source, dst):
        for d in range(1, size[axis]):
            take(axis, phase, source, dst, d)

    tok, frame = me["tok"], me["frame"]
    for e in range(experts):
        counts_ref[e] = jnp.broadcast_to(own_counts_ref[e : e + 1, :], (8, 128))
    send_all("frame", 0, lambda p: counts_ref.at[p], count_in)
    count_in[frame] = counts_ref[frame]

    def part(t, h):
        return (t * heads + h, lambda p: qkv_out.at[t, p, h], qkv_in.at[t, :, h])

    for t, ref in enumerate((k_ref, q_ref, v_ref)):
        turned = ref[...].astype(F32).T
        for h in range(heads):
            for s in range(shards):
                base = s * cols + h * HD
                qkv_out[t, s, h] = turned[base : base + HD].astype(BF)
            if h == 0:
                send_all("head", *part(t, h))
    for h in range(1, heads):
        for t in range(3):
            send_all("head", *part(t, h))
    for t in range(3):
        qkv_in[t, tok] = qkv_out[t, tok]

    token = lax.broadcasted_iota(jnp.int32, (slots, frame_tokens), 1)
    for e in range(experts):
        used = lax.broadcasted_iota(jnp.int32, (1, slots), 1) < counts_ref[e][0:1, 0:slots]
        spot = jnp.where(used, picked_ref[e], -1).astype(F32)
        column = jnp.broadcast_to(spot, (128, slots)).T[:, 0:1].astype(jnp.int32)
        picks[e] = jnp.where(column == token, 1.0, 0.0).astype(BF)
    bias_columns = jnp.broadcast_to(reduce_bias_row[...], (8, shards * cols)).T
    for s in range(shards):
        reduce_bias_ref[s] = bias_columns[s * cols : (s + 1) * cols, 0:1]

    scale = math.log2(math.e) / math.sqrt(HD)
    for h in range(heads):
        for t in range(3):
            take_all("head", *part(t, h))
        keys = jnp.concatenate([qkv_in[0, s, h] for s in range(shards)], axis=1).T
        values = jnp.concatenate([qkv_in[2, s, h] for s in range(shards)], axis=1)

        def block(j, carry):
            scores = dot(keys, qkv_in[1, j, h], 1, 0)
            top = jnp.max(scores, axis=0, keepdims=True)
            powers = jnp.exp2((scores - top) * scale)
            denominator = jnp.sum(powers, axis=0, keepdims=True)
            out = dot(values, powers.astype(BF), 1, 0)
            att_out[j, h] = (out / denominator).astype(BF)
            return carry

        lax.fori_loop(0, shards, block, 0)
        send_all("head", 3 * heads + h, lambda p: att_out.at[p, h], att_in.at[:, h])
        att_in[tok, h] = att_out[tok, h]

    take_all("frame", 0, lambda p: counts_ref.at[p], count_in)
    row = lax.broadcasted_iota(jnp.int32, (CAP, slots), 0)
    slot = lax.broadcasted_iota(jnp.int32, (CAP, slots), 1)
    first = jnp.zeros((1, slots), jnp.int32)
    for g in range(frames):
        number = count_in[g][0:1, 0:slots]
        pack = jnp.where((row == first + slot) & (slot < number), 1.0, 0.0)
        packs[g] = pack.astype(BF)
        packs_turned[g] = pack.T.astype(BF)
        first = first + number
    loads[0].wait()

    def project(q):
        block = jnp.concatenate([att_in[q, h].astype(F32) for h in range(heads)], axis=0)
        return dot(block.T.astype(BF), wo[q], 1, 0)

    projected = project(tok)
    for d in range(1, shards):
        for h in range(heads):
            q = take("head", 3 * heads + h, lambda p: att_out.at[p, h], att_in.at[:, h], d)
        projected += project(q)
    projected += out_bias_ref[...].reshape(1, shards * cols)
    residual = (stream_ref[...].astype(F32) + mod_ref[0:1] * projected).astype(BF)
    wide = residual.astype(F32)
    centred = wide - jnp.mean(wide, axis=1, keepdims=True)
    variance = jnp.mean(centred * centred, axis=1, keepdims=True)
    normed = (
        centred * lax.rsqrt(variance + 1e-06) * (1.0 + mod_ref[2:3]) + mod_ref[1:2]
    ).astype(BF)
    turned = normed.T
    for s in range(shards):
        normed_out[s] = turned[s * cols : (s + 1) * cols]
    send_all("tok", 1, lambda p: normed_out.at[p], normed_in)
    o_ref[...] = residual
    gates = dot(router_ref[...], normed, 1, 1)
    gate_out[...] = 1.0 / (1.0 + jnp.exp(-gates))
    send_all("tok", 2, lambda p: gate_out, gate_in)
    normed_in[tok] = normed_out[tok]
    gate_in[tok] = gate_out[...]

    take_all("tok", 1, lambda p: normed_out.at[p], normed_in)
    held = jnp.concatenate([normed_in[s] for s in range(shards)], axis=1)
    for d in range(1, frames + 1):
        p = lax.rem(frame + d, frames)
        put_block(chosen_out, p, dot(picks[p], held, 1, 1), slots)
        if d < frames:
            send_to("frame", 1, lambda p: chosen_out.at[p], chosen_in, d)
    rows = dot(packs[frame], get_block(chosen_out, frame, slots, cols), 1, 0)
    for d in range(1, frames):
        g = take("frame", 1, lambda p: chosen_out.at[p], chosen_in, d)
        rows += dot(packs[g], get_block(chosen_in, g, slots, cols), 1, 0)
    rows_all[tok] = rows.T.astype(BF)
    send_all("tok", 3, lambda p: rows_all.at[tok], rows_all)
    loads[1].wait()
    loads[2].wait()
    hidden = dot(rows_all[tok].T, we[tok], 1, 0)
    for d in range(1, shards):
        q = take("tok", 3, lambda p: rows_all.at[tok], rows_all, d)
        hidden += dot(rows_all[q].T, we[q], 1, 0)
    hidden = gelu(hidden + expand_bias_ref[...]).astype(BF)
    partial_out = dot(hidden, wr[...], 1, 0).T
    for s in range(shards):
        part_out[s] = partial_out[s * cols : (s + 1) * cols].astype(BF)
    send_all("tok", 4, lambda p: part_out.at[p], part_in)
    part_in[tok] = part_out[tok]
    take_all("tok", 4, lambda p: part_out.at[p], part_in)
    total = part_in[0].astype(F32)
    for s in range(1, shards):
        total += part_in[s].astype(F32)
    expert_out = (total + reduce_bias_ref[tok]).astype(BF)
    for d in range(1, frames + 1):
        p = lax.rem(frame + d, frames)
        put_block(ret_out, p, dot(packs_turned[p], expert_out, 1, 1), slots)
        if d < frames:
            send_to("frame", 2, lambda p: ret_out.at[p], ret_in, d)
    take_all("tok", 2, lambda p: gate_out, gate_in)
    gate_all = jnp.concatenate([gate_in[s] for s in range(shards)], axis=1).astype(BF)
    for e in range(experts):
        picks[e] = picks[e] * gate_all[e : e + 1]
    mixed = dot(get_block(ret_out, frame, slots, cols).T, picks[frame], 1, 0)
    for d in range(1, frames):
        e = take("frame", 2, lambda p: ret_out.at[p], ret_in, d)
        mixed += dot(get_block(ret_in, e, slots, cols).T, picks[e], 1, 0)
    for s in range(shards):
        mix_out[s] = mixed[:, s * tokens : (s + 1) * tokens].astype(BF)
    send_all("tok", 5, lambda p: mix_out.at[p], mix_in)
    mix_in[tok] = mix_out[tok]
    take_all("tok", 5, lambda p: mix_out.at[p], mix_in)
    mix = jnp.concatenate([mix_in[s].astype(F32) for s in range(shards)], axis=0).T
    o_ref[...] = (o_ref[...].astype(F32) + mod_ref[3:4] * mix).astype(BF)
    for made in sent:
        made.wait_send()


def per_device(
    stream,
    queries,
    key_vectors,
    value_vectors,
    modulation,
    output_weight,
    output_bias,
    router_weight,
    expand_weight,
    expand_bias,
    reduce_weight,
    reduce_bias,
    counts,
    picked_rows,
):
    shards = lax.axis_size("tok")
    frames = lax.axis_size("frame")
    tokens = stream.shape[1]
    width = stream.shape[2]
    hidden = expand_weight.shape[2]
    cols = width // shards
    heads = H // shards
    experts, _, slots = picked_rows.shape

    vmem = pl.BlockSpec(memory_space=pltpu.VMEM)
    hbm = pl.BlockSpec(memory_space=pl.ANY)
    layer_out = pl.pallas_call(
        layer_kernel,
        out_shape=jax.ShapeDtypeStruct((tokens, width), BF),
        in_specs=[vmem] * 11 + [hbm] * 3,
        out_specs=vmem,
        scratch_shapes=[
            pltpu.VMEM((shards, cols, width), BF),
            pltpu.VMEM((shards, cols, hidden), BF),
            pltpu.VMEM((hidden, width), BF),
            pltpu.VMEM((3, shards, heads, HD, tokens), BF),
            pltpu.VMEM((3, shards, heads, HD, tokens), BF),
            pltpu.VMEM((shards, heads, HD, tokens), BF),
            pltpu.VMEM((shards, heads, HD, tokens), BF),
            pltpu.VMEM((experts, slots, shards * tokens), BF),
            pltpu.VMEM((frames, CAP, slots), BF),
            pltpu.VMEM((frames, slots, CAP), BF),
            pltpu.VMEM((shards, cols, tokens), BF),
            pltpu.VMEM((shards, cols, tokens), BF),
            pltpu.VMEM((experts, tokens), F32),
            pltpu.VMEM((shards, experts, tokens), F32),
            pltpu.VMEM((shards, cols, 1), F32),
            pltpu.VMEM((frames, 8, 128), jnp.int32),
            pltpu.VMEM((frames, 8, 128), jnp.int32),
            pltpu.VMEM((frames, *packed_shape(slots, cols)), BF),
            pltpu.VMEM((frames, *packed_shape(slots, cols)), BF),
            pltpu.VMEM((shards, cols, CAP), BF),
            pltpu.VMEM((shards, cols, CAP), BF),
            pltpu.VMEM((shards, cols, CAP), BF),
            pltpu.VMEM((frames, *packed_shape(slots, cols)), BF),
            pltpu.VMEM((frames, *packed_shape(slots, cols)), BF),
            pltpu.VMEM((shards, cols, tokens), BF),
            pltpu.VMEM((shards, cols, tokens), BF),
            pltpu.SemaphoreType.DMA((3,)),
            pltpu.SemaphoreType.DMA((4 * heads, shards)),
            pltpu.SemaphoreType.DMA((4 * heads, shards)),
            pltpu.SemaphoreType.DMA((6, shards)),
            pltpu.SemaphoreType.DMA((6, shards)),
            pltpu.SemaphoreType.DMA((3, frames)),
            pltpu.SemaphoreType.DMA((3, frames)),
        ],
        compiler_params=pltpu.CompilerParams(
            collective_id=1, has_side_effects=True, vmem_limit_bytes=56 << 20
        ),
    )(
        queries[0],
        key_vectors[0],
        value_vectors[0],
        stream[0],
        modulation[0],
        output_bias,
        router_weight.T,
        expand_bias,
        reduce_bias,
        counts,
        picked_rows,
        output_weight.reshape(shards, cols, width),
        expand_weight[0].reshape(shards, cols, hidden),
        reduce_weight[0],
    )
    return layer_out[None]


def solution(mesh):
    return jax.shard_map(
        per_device,
        mesh=mesh,
        in_specs=(
            P("frame", "tok", None),
            P("frame", "tok", None),
            P("frame", "tok", None),
            P("frame", "tok", None),
            P("frame", None, None),
            P(),
            P(),
            P(),
            P("frame", None, "tok"),
            P("frame", "tok"),
            P("frame", "tok", None),
            P("frame", None),
            P(None, "frame"),
            P(None, "frame", None),
        ),
        out_specs=P("frame", "tok", None),
        check_vma=False,
    )
```
